32 devices in a mesh: tile: 8 (over z, x), slab: 4 (over y, core).
Axes of the slice: x: 2, y: 2, z: 4, core: 2. Of those that a mesh axis runs over, the one named last changes fastest.
Arguments:
- object_field: bfloat16 [2, 8, 1024, 512], P(None, 'slab', 'tile')
- probe_wave: bfloat16 [2, 128, 128], replicated, may hold values from -6 to 6
- prop_phase: float32 [128, 128], replicated, may hold values from -3.140625 to 3.140625
- intensity: float32 [16, 128, 128], P('tile'), may hold values from 0 to 4
- patch_rows: int32 [16], replicated, may hold values from 0 to 127
- patch_cols: int32 [16], replicated, may hold values from 0 to 384
Outputs:
- grad_object: bfloat16 [2, 8, 1024, 512], P(None, 'slab', 'tile')
The draws below stay inside these ranges and needn't reach their ends.
Inputs may be any that keep to these rules, and one draw needn't show every extreme that they name: `patch_rows`: a window of tile t covers rows of tile t and of the next tile (the first tile after the last).
All inputs are finite; a program needn't handle non-finite values.
Results may differ from the reference program's by a relative error of at most 0.005.
Values may be sent and summed in bfloat16 or wider, within the bound.
A program may use at most 64 MiB of HBM per device.

```python
import math
import jax
import jax.numpy as jnp
from jax import lax

WIN = 128
OCOL = 512
POS_DEV = 2
SLICES = 8
ROWS = 1024
POS = 16
N_TILE = 8


def draw_object_field(key, part):
    amp_key, phase_key = jax.random.split(jax.random.fold_in(key, 11))
    field_shape = (SLICES, ROWS, OCOL)
    magnitude = 0.9 + 0.2 * jax.random.uniform(amp_key, field_shape, jnp.float32)
    phases = jax.random.uniform(phase_key, field_shape, jnp.float32, -math.pi, math.pi)
    return jnp.stack([magnitude * jnp.cos(phases), magnitude * jnp.sin(phases)]).astype(jnp.bfloat16)


def touch_ends(result, rng, least, top_value):
    shape = result.shape
    index_at = [jax.random.randint(jax.random.fold_in(rng, axis), (), 0, shape[axis]) for axis in range(len(shape))]
    result = result.at[tuple(index_at)].set(least)
    longest = shape.index(max(shape))
    index_at[longest] = (index_at[longest] + 1) % shape[longest]
    return result.at[tuple(index_at)].set(top_value)


def levels(rng, extent, pieces, low, largest):
    def one(dim, parts):
        draws = jax.random.uniform(jax.random.fold_in(jax.random.fold_in(rng, 6), dim), (parts,), jnp.float32, low / len(pieces), largest / len(pieces))
        return jnp.repeat(jnp.exp(draws), extent[dim] // parts).reshape((-1,) + (1,) * (len(extent) - dim - 1))

    level = one(*pieces[0])
    for cut in pieces[1:]:
        level = level * one(*cut)
    return level


def bell_draw(own_key, dims, width, bound, kind=jnp.bfloat16):
    return jnp.clip(width * jax.random.normal(own_key, dims, jnp.float32), -bound, bound).astype(kind)


def setup_inputs(seed: int = 0) -> dict:
    key_list = jax.random.split(jax.random.key(seed), 7)
    return {
        "object_field": draw_object_field(jax.random.fold_in(key_list[6], 71), 0),
        "probe_wave": bell_draw(key_list[1], (2, WIN, WIN), 1.0, 6.0),
        "prop_phase": jnp.clip(jax.random.uniform(key_list[2], (WIN, WIN), jnp.float32, -3.140625, 3.140625), -3.140625, 3.140625),
        "intensity": jnp.clip(4.0 * jax.random.uniform(key_list[3], (POS, WIN, WIN), jnp.float32) ** levels(key_list[3], (POS, WIN, WIN), ((0, 8),), -0.2, 0.2), 0.0, 4.0),
        "patch_rows": touch_ends(jax.random.randint(key_list[4], (POS,), 0, WIN), jax.random.fold_in(key_list[4], 1), 0, WIN - 1).astype(jnp.int32),
        "patch_cols": touch_ends(jax.random.randint(key_list[5], (POS,), 0, OCOL - WIN + 1), jax.random.fold_in(key_list[5], 1), 0, OCOL - WIN).astype(jnp.int32),
    }


def fourier_tables(window, exponent_sign):
    indices = jnp.arange(window, dtype=jnp.int32)
    product = indices[:, None] * indices[None, :] % window
    angles = product.astype(jnp.float32) * (exponent_sign * 2.0 * math.pi / window)
    scaling = 1.0 / math.sqrt(window)
    real_part = jnp.cos(angles) * scaling
    imag_part = jnp.sin(angles) * scaling
    left_table = jnp.concatenate([real_part, imag_part], axis=0)
    right_table = jnp.concatenate([jnp.concatenate([real_part, imag_part], axis=1), jnp.concatenate([-imag_part, real_part], axis=1)], axis=0)
    return (left_table, right_table)

def transform(field_in, tables, window):
    left_table, right_table = tables
    first_pass = jnp.dot(field_in, right_table, precision=lax.Precision.HIGHEST, preferred_element_type=jnp.float32)
    second_pass = jnp.dot(left_table, first_pass, precision=lax.Precision.HIGHEST, preferred_element_type=jnp.float32)
    upper_half = second_pass[:window]
    lower_half = second_pass[window:]
    return jnp.concatenate([upper_half[:, :window] - lower_half[:, window:], upper_half[:, window:] + lower_half[:, :window]], axis=1)

def complex_times(left_side, right_side, window):
    left_re = left_side[..., :window].astype(jnp.float32)
    left_im = left_side[..., window:].astype(jnp.float32)
    right_re = right_side[..., :window].astype(jnp.float32)
    right_im = right_side[..., window:].astype(jnp.float32)
    return jnp.concatenate([left_re * right_re - left_im * right_im, left_re * right_im + left_im * right_re], axis=-1)

def conj_times(left_side, right_side, window):
    left_re = left_side[..., :window].astype(jnp.float32)
    left_im = left_side[..., window:].astype(jnp.float32)
    right_re = right_side[..., :window].astype(jnp.float32)
    right_im = right_side[..., window:].astype(jnp.float32)
    return jnp.concatenate([left_re * right_re + left_im * right_im, left_re * right_im - left_im * right_re], axis=-1)

def add_block(gradient, block, column, window, layers):
    zero_index = jnp.zeros((), jnp.int32)
    paired = jnp.stack([block[..., :window], block[..., window:]])
    where_at = (zero_index, zero_index, zero_index, column.astype(jnp.int32))
    current = lax.dynamic_slice(gradient, where_at, (2, layers, window, window))
    return lax.dynamic_update_slice(gradient, current + paired, where_at)

def place_rows(term_block, row_start, window, layers):
    zero_index = jnp.zeros((), jnp.int32)
    placed = jnp.zeros((layers, 2 * window, 2 * window), jnp.float32)
    return lax.dynamic_update_slice(placed, term_block, (zero_index, row_start.astype(jnp.int32), zero_index))

def reference(object_field, probe_wave, prop_phase, intensity, patch_rows, patch_cols):
    window = WIN
    forward_tables = fourier_tables(window, -1.0)
    backward_tables = fourier_tables(window, 1.0)
    propagator = jnp.concatenate([jnp.cos(prop_phase), jnp.sin(prop_phase)], axis=1)
    incoming_start = jnp.concatenate([probe_wave[0], probe_wave[1]], axis=1).astype(jnp.float32)
    offsets = jnp.arange(window, dtype=jnp.int32)

    def one_position(position):
        tile_index = position // POS_DEV
        row_index = (tile_index * window + patch_rows[position] + offsets) % ROWS
        picked = jnp.take(object_field, row_index, axis=2)
        cut_window = lax.dynamic_slice_in_dim(picked, patch_cols[position].astype(jnp.int32), window, axis=3)
        patches = jnp.concatenate([cut_window[0], cut_window[1]], axis=2)
        incoming = incoming_start
        stored = []
        outgoing = incoming
        for layer_index in range(SLICES):
            stored.append(incoming)
            outgoing = complex_times(incoming, patches[layer_index], window)
            if layer_index < SLICES - 1:
                moved = complex_times(propagator, transform(outgoing, forward_tables, window), window)
                incoming = transform(moved, backward_tables, window)
        far_field = transform(outgoing, forward_tables, window)
        far_power = far_field[:, :window] ** 2 + far_field[:, window:] ** 2
        misfit = far_power - intensity[position]
        far_grad = jnp.concatenate([misfit, misfit], axis=1) * far_field
        out_grad = transform(far_grad, backward_tables, window)
        patch_terms = [None] * SLICES
        for layer_index in reversed(range(SLICES)):
            patch_terms[layer_index] = conj_times(stored[layer_index], out_grad, window)
            if layer_index > 0:
                in_grad = conj_times(patches[layer_index], out_grad, window)
                returned = conj_times(propagator, transform(in_grad, forward_tables, window), window)
                out_grad = transform(returned, backward_tables, window)
        return jnp.stack(patch_terms)
    grad_terms = lax.map(one_position, jnp.arange(POS, dtype=jnp.int32))

    def one_tile(tile_index):
        gradient = jnp.zeros((2, SLICES, window, OCOL), jnp.float32)
        tile_before = (tile_index + N_TILE - 1) % N_TILE
        for member in range(POS_DEV):
            own_position = tile_index * POS_DEV + member
            placed = place_rows(grad_terms[own_position], patch_rows[own_position], window, SLICES)
            gradient = add_block(gradient, placed[:, :window], patch_cols[own_position], window, SLICES)
            prior_position = tile_before * POS_DEV + member
            prior_placed = place_rows(grad_terms[prior_position], patch_rows[prior_position], window, SLICES)
            gradient = add_block(gradient, prior_placed[:, window:], patch_cols[prior_position], window, SLICES)
        return gradient.astype(jnp.bfloat16)
    tiled = lax.map(one_tile, jnp.arange(N_TILE, dtype=jnp.int32))
    return jnp.moveaxis(tiled, 0, 2).reshape(2, SLICES, ROWS, OCOL)
```

```python
import functools
import math

import jax
import jax.numpy as jnp
import numpy as np
from jax import lax
from jax.experimental import pallas as pl
from jax.experimental.pallas import tpu as pltpu
from jax.sharding import PartitionSpec as P

F32 = jnp.float32
BF16 = jnp.bfloat16


def fourier_parts(window):
    index = np.arange(window)
    angle = (index[:, None] * index[None, :] % window) * (-2.0 * math.pi / window)
    real = np.cos(angle) / math.sqrt(window)
    imag = np.sin(angle) / math.sqrt(window)
    big = np.block([[real, imag], [-imag, real]]).astype(np.float32)
    high = big.astype(BF16)
    low = (big - high.astype(np.float32)).astype(BF16)
    return np.concatenate([high, high, low], axis=0)


def split(value):
    high = value.astype(BF16)
    return high, (value - high.astype(F32)).astype(BF16)


def from_right(field, right, window):
    high, low = split(jnp.concatenate(field, axis=1))
    lhs = jnp.concatenate([high, low, high], axis=1)
    rows = lhs.shape[0] // 2
    table = right[...]
    product = jnp.concatenate(
        [
            jnp.dot(lhs[:rows], table, preferred_element_type=F32),
            jnp.dot(lhs[rows:], table, preferred_element_type=F32),
        ],
        axis=0,
    )
    return product[:, :window], product[:, window:]


def transform(field, right, window):
    first = [from_right(f, right, window) for f in field]
    return [from_right((re.T, im.T), right, window) for re, im in first]


def times(a, b):
    return a[0] * b[0] - a[1] * b[1], a[0] * b[1] + a[1] * b[0]


def conj_times(a, b):
    return a[0] * b[0] + a[1] * b[1], a[0] * b[1] - a[1] * b[0]


def conj(a):
    return a[0], -a[1]


MESH = pl.DeviceIdType.MESH


def one_hot(shape, along, offset):
    here = lax.broadcasted_iota(jnp.int32, shape, along)
    there = lax.broadcasted_iota(jnp.int32, shape, 1 - along)
    return jnp.where(here == there + offset, 1.0, 0.0).astype(BF16)


def halves(block, window):
    return block[:, :window], block[:, window:]


def wide(field):
    return jnp.concatenate(field, axis=1)


def kernel(
    tiles, sections, row_ref, col_ref, obj, probe, phase, measured, right_in, out,
    place, cut_low, cut_high, cut_give, both, patches, psi, work, prop, seen, turned, stage, landed, right,
    low_send, high_send, give_send, part_recv, give_recv, cross_send, cross_recv,
    seen_send, seen_recv, near_send, near_recv, far_send, far_recv, table_sem,
):
    layers, window, columns = obj.shape[1], obj.shape[2], obj.shape[3]
    count, slices = measured.shape[0], patches.shape[0]
    half = count // 2
    groups = sections // 2
    owned = 2 * layers
    last = slices - 1
    tile = lax.axis_index("tile")
    slab = lax.axis_index("slab")
    after, prior = lax.rem(tile + 1, tiles), lax.rem(tile + tiles - 1, tiles)
    group, side = slab // 2, lax.rem(slab, 2)
    partner = slab + 1 - 2 * side
    first_own = group * owned
    base = jnp.where(side == 0, tile, prior)
    beyond = jnp.where(side == 0, after, prior)

    def remote(src, dst, send, recv, **device):
        return pltpu.make_async_remote_copy(
            src_ref=src, dst_ref=dst, send_sem=send, recv_sem=recv,
            device_id=device, device_id_type=MESH,
        )

    barrier = pltpu.get_barrier_semaphore()
    greeted = [{"tile": to, "slab": 2 * group + s} for to in (after, prior) for s in range(2)]
    greeted.append({"slab": partner})
    for step in range(1, groups):
        greeted.append({"slab": lax.rem(group + step, groups) * 2 + side})
    for device in greeted:
        pl.semaphore_signal(barrier, inc=1, device_id=device, device_id_type=MESH)
    table = pltpu.make_async_copy(right_in, right, table_sem)
    table.start()

    starts = [prior * count, tile * count + half, tile * count, prior * count + half]
    for slot, start in enumerate(starts):
        for q in range(half):
            place[slot, q] = one_hot((window, columns), 1, col_ref[start + q])

    def cut(layer, pick):
        rows = jnp.concatenate([obj[0, layer], obj[1, layer]], axis=0)
        got = lax.dot_general(
            rows, pick, (((1,), (1,)), ((), ())), preferred_element_type=F32
        ).astype(BF16)
        return wide((got[:window], got[window:]))

    def low_copy(layer, q):
        return remote(
            cut_low.at[layer, q], both.at[side * layers + layer, q, 1],
            low_send.at[layer, q], part_recv.at[side * layers + layer, q],
            tile=prior, slab=2 * group,
        )

    def high_copy(layer, q):
        return remote(
            cut_high.at[layer, q], both.at[side * layers + layer, q, 0],
            high_send.at[layer, q], part_recv.at[side * layers + layer, q],
            tile=after, slab=2 * group + 1,
        )

    def give_copy(layer, q):
        return remote(
            cut_give.at[layer, q], both.at[side * layers + layer, q, 1 - side],
            give_send.at[layer, q], give_recv.at[layer, q], slab=partner,
        )

    def seen_copy(q):
        return remote(
            measured.at[half + q], seen.at[q], seen_send.at[q], seen_recv.at[q], tile=after
        )

    for layer in range(layers):
        for q in range(half):
            cut_low[layer, q] = cut(layer, place[0, q])
            cut_high[layer, q] = cut(layer, place[1, q])
        if layer == 0:
            pl.semaphore_wait(barrier, len(greeted))
        for q in range(half):
            low_copy(layer, q).start()
            high_copy(layer, q).start()
    for layer in range(layers):
        for q in range(half):
            cut_give[layer, q] = cut(layer, place[3 - side, q])
            give_copy(layer, q).start()
    for layer in range(layers):
        for q in range(half):
            both[side * layers + layer, q, side] = cut(layer, place[2 + side, q])

    @pl.when(side == 1)
    def _():
        for q in range(half):
            seen_copy(q).start()

    my_rows = [row_ref[base * count + side * half + q] for q in range(half)]
    phase_turned = phase[...].T
    prop[...] = wide((jnp.cos(phase_turned), jnp.sin(phase_turned)))

    def cross_copy(step, at):
        block = patches.at[first_own + at]
        return remote(
            block, block, cross_send.at[step - 1, at], cross_recv.at[step - 1, at],
            slab=lax.rem(group + step, groups) * 2 + side,
        )

    def cross_arrival(step, j, at):
        block = patches.at[j]
        return remote(
            block, block, cross_send.at[step - 1, at], cross_recv.at[step - 1, at],
            slab=lax.rem(group + step, groups) * 2 + side,
        )

    def take_rows(at):
        owner = at // layers
        for q in range(half):
            remote(
                cut_low.at[0, q], both.at[at, q, 1 - side],
                low_send.at[0, q], part_recv.at[at, q], slab=partner,
            ).wait_recv()

        @pl.when(owner != side)
        def _():
            for q in range(half):
                layer = lax.rem(at, layers)
                remote(
                    cut_give.at[0, q], both.at[at, q, side],
                    give_send.at[0, q], give_recv.at[layer, q], slab=partner,
                ).wait_recv()

        for q in range(half):
            pick = one_hot((window, 2 * window), 1, my_rows[q])
            rows = both[at, q].reshape(2 * window, 2 * window)
            patches[first_own + at, q] = jnp.dot(
                pick, rows, preferred_element_type=F32
            ).astype(BF16)
        for step in range(1, groups):
            cross_copy(step, at).start()

    @pl.when(group > 0)
    def _():
        for at in range(owned):
            take_rows(at)

    def arrive(j):
        of_group, at = j // owned, lax.rem(j, owned)
        step = lax.rem(group - of_group + groups, groups)

        @pl.when(of_group != group)
        def _():
            cross_arrival(step, j, at).wait_recv()

    table.wait()
    run = functools.partial(transform, right=right, window=window)
    start = (probe[0].astype(F32), probe[1].astype(F32))
    for q in range(half):
        psi[0, q] = wide(start)

    def patch(j):
        return [halves(patches[j, q].astype(F32), window) for q in range(half)]

    def waves(ref, j):
        return [halves(ref[j, q], window) for q in range(half)]

    def forward(j, carried):
        @pl.when((group == 0) & (j < owned))
        def _():
            take_rows(j)

        arrive(j)
        chi = [times(a, b) for a, b in zip(waves(psi, j), patch(j))]
        moved = run(chi)
        pace = halves(prop[...], window)
        back = run([conj(times(pace, f)) for f in moved])
        for q in range(half):
            psi[j + 1, q] = wide(conj(back[q]))
        return carried

    lax.fori_loop(0, last, forward, 0)

    @pl.when(side == 0)
    def _():
        for q in range(half):
            turned[q] = measured[q].T

    @pl.when(side == 1)
    def _():
        for q in range(half):
            seen_copy(q).wait_recv()
            turned[q] = seen[q].T

    @pl.when((group == 0) & (last < owned))
    def _():
        take_rows(last)

    arrive(last)
    chi = [times(a, b) for a, b in zip(waves(psi, last), patch(last))]
    far = run(chi)
    shaped = []
    for q, (re, im) in enumerate(far):
        misfit = re * re + im * im - turned[q]
        shaped.append((misfit * re, -(misfit * im)))
    grad = [conj(f) for f in run(shaped)]
    for q in range(half):
        work[q] = wide(grad[q])

    def near_copy(at, q):
        return remote(
            stage.at[at, q, side], landed.at[lax.rem(at, layers), 2 + side, q],
            near_send.at[lax.rem(at, layers), q], near_recv.at[lax.rem(at, layers), q], slab=partner,
        )

    def far_copy(at, q):
        return remote(
            stage.at[at, q, 1 - side], landed.at[lax.rem(at, layers), side, q],
            far_send.at[at, q], far_recv.at[side, lax.rem(at, layers), q],
            tile=beyond, slab=2 * group + at // layers,
        )

    def own_term(j):
        @pl.when(j < first_own + owned)
        def _():
            at = j - first_own
            for q in range(half):
                term = wide(conj_times(halves(psi[j, q], window), halves(work[q], window)))
                pick = one_hot((2 * window, window), 0, my_rows[q])
                placed = jnp.dot(
                    pick, term.astype(BF16), preferred_element_type=F32
                ).astype(BF16)
                stage[at, q] = placed.reshape(2, window, 2 * window)
                far_copy(at, q).start()

            @pl.when(at // layers != side)
            def _():
                for q in range(half):
                    near_copy(at, q).start()

    def backward(i, carried):
        j = last - i
        own_term(j)
        grads = [halves(work[q], window) for q in range(half)]
        inner = [conj_times(a, b) for a, b in zip(patch(j), grads)]
        moved = run(inner)
        pace = halves(prop[...], window)
        back = run([conj(conj_times(pace, f)) for f in moved])
        for q in range(half):
            work[q] = wide(conj(back[q]))
        return carried

    lax.fori_loop(0, last - first_own, backward, 0)
    own_term(first_own)

    def far_arrival(layer, of_side, q):
        return remote(
            stage.at[0, q, 0], landed.at[layer, of_side, q],
            far_send.at[0, q], far_recv.at[of_side, layer, q], slab=partner,
        )

    def near_arrival(layer, q):
        return remote(
            stage.at[0, q, 0], landed.at[layer, 3 - side, q],
            near_send.at[layer, q], near_recv.at[layer, q], slab=partner,
        )

    all_place = place[...].reshape(4 * half * window, columns)
    for layer in reversed(range(layers)):
        for q in range(half):
            landed[layer, 2 + side, q] = stage[side * layers + layer, q, side]
            near_arrival(layer, q).wait_recv()
            for of_side in range(2):
                far_arrival(layer, of_side, q).wait_recv()
        blocks = [halves(landed[layer, slot, q], window) for slot in range(4) for q in range(half)]
        both_parts = jnp.concatenate(
            [jnp.concatenate([b[part] for b in blocks], axis=1) for part in range(2)], axis=0
        )
        total = jnp.dot(both_parts, all_place, preferred_element_type=F32).astype(out.dtype)
        out[0, layer] = total[:window]
        out[1, layer] = total[window:]

    @pl.when(side == 1)
    def _():
        for q in range(half):
            seen_copy(q).wait_send()

    for q in range(half):
        for layer in range(layers):
            low_copy(layer, q).wait_send()
            high_copy(layer, q).wait_send()
            give_copy(layer, q).wait_send()
            near_copy((1 - side) * layers + layer, q).wait_send()
        for at in range(owned):
            far_copy(at, q).wait_send()
    for at in range(owned):
        for step in range(1, groups):
            cross_copy(step, at).wait_send()


def body(object_field, probe_wave, prop_phase, intensity, patch_rows, patch_cols):
    window = probe_wave.shape[1]
    layers, columns = object_field.shape[1], object_field.shape[3]
    half = intensity.shape[0] // 2
    tiles, sections = lax.axis_size("tile"), lax.axis_size("slab")
    slices = sections * layers
    groups = sections // 2
    owned = 2 * layers
    right = fourier_parts(window)
    block = (window, 2 * window)
    dma = pltpu.SemaphoreType.DMA
    return pl.pallas_call(
        functools.partial(kernel, tiles, sections),
        out_shape=jax.ShapeDtypeStruct(object_field.shape, BF16),
        in_specs=[pl.BlockSpec(memory_space=pltpu.SMEM)] * 2
        + [pl.BlockSpec(memory_space=pltpu.VMEM)] * 4
        + [pl.BlockSpec(memory_space=pl.ANY)],
        out_specs=pl.BlockSpec(memory_space=pltpu.VMEM),
        scratch_shapes=[
            pltpu.VMEM((4, half, window, columns), BF16),
            pltpu.VMEM((layers, half) + block, BF16),
            pltpu.VMEM((layers, half) + block, BF16),
            pltpu.VMEM((layers, half) + block, BF16),
            pltpu.VMEM((owned, half, 2) + block, BF16),
            pltpu.VMEM((slices, half) + block, BF16),
            pltpu.VMEM((slices, half) + block, F32),
            pltpu.VMEM((half,) + block, F32),
            pltpu.VMEM(block, F32),
            pltpu.VMEM((half, window, window), F32),
            pltpu.VMEM((half, window, window), F32),
            pltpu.VMEM((owned, half, 2) + block, BF16),
            pltpu.VMEM((layers, 4, half) + block, BF16),
            pltpu.VMEM(right.shape, BF16),
            dma((layers, half)),
            dma((layers, half)),
            dma((layers, half)),
            dma((owned, half)),
            dma((layers, half)),
            dma((groups - 1, owned)),
            dma((groups - 1, owned)),
            dma((half,)),
            dma((half,)),
            dma((layers, half)),
            dma((layers, half)),
            dma((owned, half)),
            dma((2, layers, half)),
            dma(()),
        ],
        compiler_params=pltpu.CompilerParams(
            collective_id=0, has_side_effects=True, vmem_limit_bytes=60 * 1024 * 1024
        ),
    )(
        patch_rows, patch_cols, object_field, probe_wave, prop_phase, intensity,
        jnp.asarray(right),
    )


def solution(mesh):
    return jax.shard_map(
        body,
        mesh=mesh,
        in_specs=(P(None, "slab", "tile", None), P(), P(), P("tile", None, None), P(), P()),
        out_specs=P(None, "slab", "tile", None),
        check_vma=False,
    )
```

```python
import functools
import math

import jax
import jax.numpy as jnp
import numpy as np
from jax import lax
from jax.experimental import pallas as pl
from jax.experimental.pallas import tpu as pltpu
from jax.sharding import PartitionSpec as P

F32 = jnp.float32
BF16 = jnp.bfloat16


def fourier_parts(window):
    index = np.arange(window)
    angle = (index[:, None] * index[None, :] % window) * (-2.0 * math.pi / window)
    real = np.cos(angle) / math.sqrt(window)
    imag = np.sin(angle) / math.sqrt(window)
    big = np.block([[real, imag], [-imag, real]]).astype(np.float32)
    high = big.astype(BF16)
    low = (big - high.astype(np.float32)).astype(BF16)
    left = np.block([[real, -imag], [imag, real]]).astype(np.float32)
    left_high = left.astype(BF16)
    left_low = (left - left_high.astype(np.float32)).astype(BF16)
    w = window
    return np.concatenate(
        [high, high, low, left_high[:w], left_low[:w], left_high[w:], left_low[w:]], axis=0
    )


def split(value):
    high = value.astype(BF16)
    return high, (value - high.astype(F32)).astype(BF16)


def from_right(field, right, window):
    high, low = split(jnp.concatenate(field, axis=1))
    wide_rows, table_rows = high.shape[0] // 2, 2 * window
    parts = []
    for at in (0, wide_rows):
        upper, lower = high[at : at + wide_rows], low[at : at + wide_rows]
        main = jnp.dot(
            jnp.concatenate([upper, lower], axis=0), right[:table_rows], preferred_element_type=F32
        )
        rest = jnp.dot(upper, right[2 * table_rows : 3 * table_rows], preferred_element_type=F32)
        parts.append(main[:wide_rows] + main[wide_rows:] + rest)
    product = jnp.concatenate(parts, axis=0)
    return product[:, :window], product[:, window:]


def from_left(field, right, window):
    high, low = split(jnp.concatenate(field, axis=0))
    data = jnp.concatenate([high, low], axis=1)
    table_rows = 2 * window
    out = []
    for part in range(2):
        rows = right[pl.ds(3 * table_rows + part * table_rows, table_rows)]
        got = jnp.dot(rows, data, preferred_element_type=F32)
        out.append(got[:window, :window] + got[:window, window:] + got[window:, :window])
    return out[0], out[1]


def transform(field, right, window):
    first = [from_right(f, right, window) for f in field]
    return [from_left(f, right, window) for f in first]


def times(a, b):
    return a[0] * b[0] - a[1] * b[1], a[0] * b[1] + a[1] * b[0]


def conj_times(a, b):
    return a[0] * b[0] + a[1] * b[1], a[0] * b[1] - a[1] * b[0]


def conj(a):
    return a[0], -a[1]


MESH = pl.DeviceIdType.MESH


def one_hot(shape, along, offset):
    here = lax.broadcasted_iota(jnp.int32, shape, along)
    there = lax.broadcasted_iota(jnp.int32, shape, 1 - along)
    return jnp.where(here == there + offset, 1.0, 0.0).astype(BF16)


def halves(block, window):
    return block[:, :window], block[:, window:]


def kernel(
    tiles, sections, row_in, col_in, obj_in, probe_in, phase_in, measured_in, right_in, out,
    row_ref, col_ref, obj, probe, phase, measured,
    place, cut_low, cut_high, cut_give, both, patches, psi, work, prop, seen, stage, landed, right,
    load_sem, obj_sem,
    low_send, high_send, give_send, part_recv, give_recv, cross_send, cross_recv,
    seen_send, seen_recv, near_send, near_recv, far_send, far_recv,
):
    layers, window, columns = obj.shape[1], obj.shape[2], obj.shape[3]
    count, slices = measured.shape[0], patches.shape[0]
    half = count // 2
    groups = sections // 2
    owned = 2 * layers
    last = slices - 1
    tile = lax.axis_index("tile")
    slab = lax.axis_index("slab")
    after, prior = lax.rem(tile + 1, tiles), lax.rem(tile + tiles - 1, tiles)
    group, side = slab // 2, lax.rem(slab, 2)
    partner = slab + 1 - 2 * side
    first_own = group * owned
    base = jnp.where(side == 0, tile, prior)
    beyond = jnp.where(side == 0, after, prior)
    pieces = [(q, c) for q in range(half) for c in range(2)]

    def remote(src, dst, send, recv, **device):
        return pltpu.make_async_remote_copy(
            src_ref=src, dst_ref=dst, send_sem=send, recv_sem=recv,
            device_id=device, device_id_type=MESH,
        )

    barrier = pltpu.get_barrier_semaphore()
    greeted = [{"tile": to, "slab": 2 * group + s} for to in (after, prior) for s in range(2)]
    greeted.append({"slab": partner})
    for step in range(1, groups):
        greeted.append({"slab": lax.rem(group + step, groups) * 2 + side})
    for device in greeted:
        pl.semaphore_signal(barrier, inc=1, device_id=device, device_id_type=MESH)

    loads = [
        pltpu.make_async_copy(src, dst, load_sem.at[k])
        for k, (src, dst) in enumerate(
            [(col_in, col_ref), (row_in, row_ref), (phase_in, phase), (probe_in, probe),
             (right_in, right), (measured_in, measured)]
        )
    ]
    obj_loads = [
        pltpu.make_async_copy(obj_in.at[:, layer], obj.at[:, layer], obj_sem.at[layer])
        for layer in range(layers)
    ]
    loads[0].start()
    for copy in obj_loads + loads[1:]:
        copy.start()

    loads[0].wait()
    starts = [prior * count, tile * count + half, tile * count, prior * count + half]
    for slot, start in enumerate(starts):
        for q in range(half):
            place[slot, q] = one_hot((window, columns), 1, col_ref[start + q])

    def cut(layer, pick, target):
        for c in range(2):
            target[c] = lax.dot_general(
                obj[c, layer], pick, (((1,), (1,)), ((), ())), preferred_element_type=F32
            ).astype(BF16)

    def low_copy(layer, q, c):
        return remote(
            cut_low.at[layer, q, c], both.at[side * layers + layer, q, c, 1],
            low_send.at[layer, q, c], part_recv.at[side * layers + layer, q, c],
            tile=prior, slab=2 * group,
        )

    def high_copy(layer, q, c):
        return remote(
            cut_high.at[layer, q, c], both.at[side * layers + layer, q, c, 0],
            high_send.at[layer, q, c], part_recv.at[side * layers + layer, q, c],
            tile=after, slab=2 * group + 1,
        )

    def give_copy(layer, q, c):
        return remote(
            cut_give.at[layer, q, c], both.at[side * layers + layer, q, c, 1 - side],
            give_send.at[layer, q, c], give_recv.at[layer, q, c], slab=partner,
        )

    def seen_copy(q):
        return remote(
            measured.at[half + q], seen.at[q], seen_send.at[q], seen_recv.at[q], tile=after
        )

    for layer in range(layers):
        obj_loads[layer].wait()
        for q in range(half):
            cut(layer, place[0, q], cut_low.at[layer, q])
            cut(layer, place[1, q], cut_high.at[layer, q])
    pl.semaphore_wait(barrier, len(greeted))
    for layer in range(layers):
        for q, c in pieces:
            low_copy(layer, q, c).start()
            high_copy(layer, q, c).start()
    for layer in range(layers):
        for q in range(half):
            cut(layer, place[3 - side, q], cut_give.at[layer, q])
        for q, c in pieces:
            give_copy(layer, q, c).start()
    for layer in range(layers):
        for q, c in pieces:
            both[side * layers + layer, q, c, side] = lax.dot_general(
                obj[c, layer], place[2 + side, q], (((1,), (1,)), ((), ())),
                preferred_element_type=F32,
            ).astype(BF16)

    for copy in loads[1:]:
        copy.wait()
    my_rows = [row_ref[base * count + side * half + q] for q in range(half)]
    prop[0] = jnp.cos(phase[...])
    prop[1] = jnp.sin(phase[...])

    def cross_copy(step, at, c):
        block = patches.at[first_own + at, c]
        return remote(
            block, block, cross_send.at[step - 1, at, c], cross_recv.at[step - 1, at, c],
            slab=lax.rem(group + step, groups) * 2 + side,
        )

    def cross_arrival(step, j, at, c):
        block = patches.at[j, c]
        return remote(
            block, block, cross_send.at[step - 1, at, c], cross_recv.at[step - 1, at, c],
            slab=lax.rem(group + step, groups) * 2 + side,
        )

    def take_rows(at, c):
        owner, layer = at // layers, lax.rem(at, layers)
        for q in range(half):
            remote(
                cut_low.at[0, q, c], both.at[at, q, c, 1 - side],
                low_send.at[0, q, c], part_recv.at[at, q, c], slab=partner,
            ).wait_recv()

        @pl.when(owner != side)
        def _():
            for q in range(half):
                remote(
                    cut_give.at[0, q, c], both.at[at, q, c, side],
                    give_send.at[0, q, c], give_recv.at[layer, q, c], slab=partner,
                ).wait_recv()

        for q in range(half):
            pick = one_hot((window, 2 * window), 1, my_rows[q])
            rows = both[at, q, c].reshape(2 * window, window)
            patches[first_own + at, c, q] = jnp.dot(
                pick, rows, preferred_element_type=F32
            ).astype(BF16)
        for step in range(1, groups):
            cross_copy(step, at, c).start()

    @pl.when(group > 0)
    def _():
        for layer in range(layers):
            for c in range(2):
                for owner in range(2):
                    take_rows(owner * layers + layer, c)

    def arrive(j):
        of_group, at = j // owned, lax.rem(j, owned)
        step = lax.rem(group - of_group + groups, groups)

        @pl.when(of_group != group)
        def _():
            for c in range(2):
                cross_arrival(step, j, at, c).wait_recv()

    run = functools.partial(transform, right=right, window=window)
    for q in range(half):
        for c in range(2):
            psi[0, q, c] = probe[c].astype(F32)

    def patch(j):
        return [(patches[j, 0, q].astype(F32), patches[j, 1, q].astype(F32)) for q in range(half)]

    def pair(ref, q):
        return ref[q, 0], ref[q, 1]

    def waves(j):
        return [(psi[j, q, 0], psi[j, q, 1]) for q in range(half)]

    def forward(j, carried):
        @pl.when((group == 0) & (j < layers))
        def _():
            for c in range(2):
                take_rows(j, c)
                take_rows(j + layers, c)

        @pl.when((side == 1) & (j == layers))
        def _():
            for q in range(half):
                seen_copy(q).start()

        arrive(j)
        chi = [times(a, b) for a, b in zip(waves(j), patch(j))]
        moved = run(chi)
        pace = (prop[0], prop[1])
        back = run([conj(times(pace, f)) for f in moved])
        for q in range(half):
            psi[j + 1, q, 0] = back[q][0]
            psi[j + 1, q, 1] = -back[q][1]
        return carried

    lax.fori_loop(0, last, forward, 0)

    @pl.when(side == 0)
    def _():
        for q in range(half):
            seen[q] = measured[q]

    @pl.when(side == 1)
    def _():
        for q in range(half):
            seen_copy(q).wait_recv()

    arrive(last)
    chi = [times(a, b) for a, b in zip(waves(last), patch(last))]
    far = run(chi)
    shaped = []
    for q, (re, im) in enumerate(far):
        misfit = re * re + im * im - seen[q]
        shaped.append((misfit * re, -(misfit * im)))
    grad = [conj(f) for f in run(shaped)]
    for q in range(half):
        work[q, 0], work[q, 1] = grad[q]

    def near_copy(at, q):
        return remote(
            stage.at[at, q, side], landed.at[lax.rem(at, layers), 2 + side, q],
            near_send.at[lax.rem(at, layers), q], near_recv.at[lax.rem(at, layers), q], slab=partner,
        )

    def far_copy(at, q):
        return remote(
            stage.at[at, q, 1 - side], landed.at[lax.rem(at, layers), side, q],
            far_send.at[at, q], far_recv.at[side, lax.rem(at, layers), q],
            tile=beyond, slab=2 * group + at // layers,
        )

    def own_term(j):
        @pl.when(j < first_own + owned)
        def _():
            at = j - first_own
            for q in range(half):
                term = jnp.concatenate(
                    conj_times((psi[j, q, 0], psi[j, q, 1]), pair(work, q)), axis=1
                )
                pick = one_hot((2 * window, window), 0, my_rows[q])
                placed = jnp.dot(
                    pick, term.astype(BF16), preferred_element_type=F32
                ).astype(BF16)
                for part in range(2):
                    rows = placed[part * window : (part + 1) * window]
                    stage[at, q, part, 0], stage[at, q, part, 1] = halves(rows, window)
                far_copy(at, q).start()

            @pl.when(at // layers != side)
            def _():
                for q in range(half):
                    near_copy(at, q).start()

    def backward(i, carried):
        j = last - i
        own_term(j)
        grads = [pair(work, q) for q in range(half)]
        inner = [conj_times(a, b) for a, b in zip(patch(j), grads)]
        moved = run(inner)
        pace = (prop[0], prop[1])
        back = run([conj(conj_times(pace, f)) for f in moved])
        for q in range(half):
            work[q, 0] = back[q][0]
            work[q, 1] = -back[q][1]
        return carried

    lax.fori_loop(0, last - first_own, backward, 0)
    own_term(first_own)

    def far_arrival(layer, of_side, q):
        return remote(
            stage.at[0, q, 0], landed.at[layer, of_side, q],
            far_send.at[0, q], far_recv.at[of_side, layer, q], slab=partner,
        )

    def near_arrival(layer, q):
        return remote(
            stage.at[0, q, 0], landed.at[layer, 3 - side, q],
            near_send.at[layer, q], near_recv.at[layer, q], slab=partner,
        )

    all_place = place[...].reshape(4 * half * window, columns)
    for layer in reversed(range(layers)):
        for q in range(half):
            landed[layer, 2 + side, q] = stage[side * layers + layer, q, side]
            near_arrival(layer, q).wait_recv()
            for of_side in range(2):
                far_arrival(layer, of_side, q).wait_recv()
        for c in range(2):
            blocks = [landed[layer, slot, q, c] for slot in range(4) for q in range(half)]
            out[c, layer] = jnp.dot(
                jnp.concatenate(blocks, axis=1), all_place, preferred_element_type=F32
            ).astype(out.dtype)

    @pl.when(side == 1)
    def _():
        for q in range(half):
            seen_copy(q).wait_send()

    for layer in range(layers):
        for q, c in pieces:
            low_copy(layer, q, c).wait_send()
            high_copy(layer, q, c).wait_send()
            give_copy(layer, q, c).wait_send()
        for q in range(half):
            near_copy((1 - side) * layers + layer, q).wait_send()
    for at in range(owned):
        for q in range(half):
            far_copy(at, q).wait_send()
        for c in range(2):
            for step in range(1, groups):
                cross_copy(step, at, c).wait_send()


def body(object_field, probe_wave, prop_phase, intensity, patch_rows, patch_cols):
    window = probe_wave.shape[1]
    layers, columns = object_field.shape[1], object_field.shape[3]
    half = intensity.shape[0] // 2
    tiles, sections = lax.axis_size("tile"), lax.axis_size("slab")
    slices = sections * layers
    groups = sections // 2
    owned = 2 * layers
    right = fourier_parts(window)
    block = (window, window)
    dma = pltpu.SemaphoreType.DMA
    return pl.pallas_call(
        functools.partial(kernel, tiles, sections),
        out_shape=jax.ShapeDtypeStruct(object_field.shape, BF16),
        in_specs=[pl.BlockSpec(memory_space=pl.ANY)] * 7,
        out_specs=pl.BlockSpec(memory_space=pltpu.VMEM),
        scratch_shapes=[
            pltpu.SMEM(patch_rows.shape, jnp.int32),
            pltpu.SMEM(patch_cols.shape, jnp.int32),
            pltpu.VMEM(object_field.shape, BF16),
            pltpu.VMEM(probe_wave.shape, BF16),
            pltpu.VMEM(prop_phase.shape, F32),
            pltpu.VMEM(intensity.shape, F32),
            pltpu.VMEM((4, half, window, columns), BF16),
            pltpu.VMEM((layers, half, 2) + block, BF16),
            pltpu.VMEM((layers, half, 2) + block, BF16),
            pltpu.VMEM((layers, half, 2) + block, BF16),
            pltpu.VMEM((owned, half, 2, 2) + block, BF16),
            pltpu.VMEM((slices, 2, half) + block, BF16),
            pltpu.VMEM((slices, half, 2) + block, F32),
            pltpu.VMEM((half, 2) + block, F32),
            pltpu.VMEM((2,) + block, F32),
            pltpu.VMEM((half,) + block, F32),
            pltpu.VMEM((owned, half, 2, 2) + block, BF16),
            pltpu.VMEM((layers, 4, half, 2) + block, BF16),
            pltpu.VMEM(right.shape, BF16),
            dma((6,)),
            dma((layers,)),
            dma((layers, half, 2)),
            dma((layers, half, 2)),
            dma((layers, half, 2)),
            dma((owned, half, 2)),
            dma((layers, half, 2)),
            dma((groups - 1, owned, 2)),
            dma((groups - 1, owned, 2)),
            dma((half,)),
            dma((half,)),
            dma((layers, half)),
            dma((layers, half)),
            dma((owned, half)),
            dma((2, layers, half)),
        ],
        compiler_params=pltpu.CompilerParams(
            collective_id=0, has_side_effects=True, vmem_limit_bytes=60 * 1024 * 1024
        ),
    )(
        patch_rows, patch_cols, object_field, probe_wave, prop_phase, intensity,
        jnp.asarray(right),
    )


def solution(mesh):
    return jax.shard_map(
        body,
        mesh=mesh,
        in_specs=(P(None, "slab", "tile", None), P(), P(), P("tile", None, None), P(), P()),
        out_specs=P(None, "slab", "tile", None),
        check_vma=False,
    )
```

```python
import functools
import math

import jax
import jax.numpy as jnp
import numpy as np
from jax import lax
from jax.experimental import pallas as pl
from jax.experimental.pallas import tpu as pltpu
from jax.sharding import PartitionSpec as P

F32 = jnp.float32
BF16 = jnp.bfloat16


def fourier_parts(window):
    index = np.arange(window)
    angle = (index[:, None] * index[None, :] % window) * (-2.0 * math.pi / window)
    real = np.cos(angle) / math.sqrt(window)
    imag = np.sin(angle) / math.sqrt(window)
    big = np.block([[real, imag], [-imag, real]]).astype(np.float32)
    high = big.astype(BF16)
    low = (big - high.astype(np.float32)).astype(BF16)
    left = np.block([[real, -imag], [imag, real]]).astype(np.float32)
    left_high = left.astype(BF16)
    left_low = (left - left_high.astype(np.float32)).astype(BF16)
    w = window
    return np.concatenate(
        [high, high, low, left_high[:w], left_low[:w], left_high[w:], left_low[w:]], axis=0
    )


def split(value):
    high = value.astype(BF16)
    return high, (value - high.astype(F32)).astype(BF16)


def from_right(field, right, window):
    high, low = split(jnp.concatenate(field, axis=1))
    wide_rows, table_rows = high.shape[0] // 2, 2 * window
    parts = []
    for at in (0, wide_rows):
        upper, lower = high[at : at + wide_rows], low[at : at + wide_rows]
        main = jnp.dot(
            jnp.concatenate([upper, lower], axis=0), right[:table_rows], preferred_element_type=F32
        )
        rest = jnp.dot(upper, right[2 * table_rows : 3 * table_rows], preferred_element_type=F32)
        parts.append(main[:wide_rows] + main[wide_rows:] + rest)
    product = jnp.concatenate(parts, axis=0)
    return product[:, :window], product[:, window:]


def from_left(field, right, window):
    high, low = split(jnp.concatenate(field, axis=0))
    data = jnp.concatenate([high, low], axis=1)
    table_rows = 2 * window
    out = []
    for part in range(2):
        rows = right[pl.ds(3 * table_rows + part * table_rows, table_rows)]
        got = jnp.dot(rows, data, preferred_element_type=F32)
        out.append(got[:window, :window] + got[:window, window:] + got[window:, :window])
    return out[0], out[1]


def transform(field, right, window):
    first = [from_right(f, right, window) for f in field]
    return [from_left(f, right, window) for f in first]


def times(a, b):
    return a[0] * b[0] - a[1] * b[1], a[0] * b[1] + a[1] * b[0]


def conj_times(a, b):
    return a[0] * b[0] + a[1] * b[1], a[0] * b[1] - a[1] * b[0]


def conj(a):
    return a[0], -a[1]


MESH = pl.DeviceIdType.MESH


def one_hot(shape, along, offset):
    here = lax.broadcasted_iota(jnp.int32, shape, along)
    there = lax.broadcasted_iota(jnp.int32, shape, 1 - along)
    return jnp.where(here == there + offset, 1.0, 0.0).astype(BF16)


def halves(block, window):
    return block[:, :window], block[:, window:]


def kernel(
    tiles, sections, row_in, col_in, obj_in, probe_in, phase_in, measured_in, right_in, out,
    row_ref, col_ref, obj, probe, phase, measured,
    place, cut_low, cut_high, cut_give, both, patches, psi, work, prop, seen, stage, landed, right,
    total, load_sem, obj_sem, out_sem,
    low_send, high_send, give_send, part_recv, give_recv, cross_send, cross_recv,
    seen_send, seen_recv, near_send, near_recv, far_send, far_recv,
):
    layers, window, columns = obj.shape[1], obj.shape[2], obj.shape[3]
    count, slices = measured.shape[0], patches.shape[0]
    half = count // 2
    groups = sections // 2
    owned = 2 * layers
    last = slices - 1
    tile = lax.axis_index("tile")
    slab = lax.axis_index("slab")
    after, prior = lax.rem(tile + 1, tiles), lax.rem(tile + tiles - 1, tiles)
    group, side = slab // 2, lax.rem(slab, 2)
    partner = slab + 1 - 2 * side
    first_own = group * owned
    base = jnp.where(side == 0, tile, prior)
    beyond = jnp.where(side == 0, after, prior)
    pieces = [(q, c) for q in range(half) for c in range(2)]

    def remote(src, dst, send, recv, **device):
        return pltpu.make_async_remote_copy(
            src_ref=src, dst_ref=dst, send_sem=send, recv_sem=recv,
            device_id=device, device_id_type=MESH,
        )

    barrier = pltpu.get_barrier_semaphore()
    greeted = [{"tile": to, "slab": 2 * group + s} for to in (after, prior) for s in range(2)]
    greeted.append({"slab": partner})
    for step in range(1, groups):
        greeted.append({"slab": lax.rem(group + step, groups) * 2 + side})
    for device in greeted:
        pl.semaphore_signal(barrier, inc=1, device_id=device, device_id_type=MESH)

    loads = [
        pltpu.make_async_copy(src, dst, load_sem.at[k])
        for k, (src, dst) in enumerate(
            [(col_in, col_ref), (row_in, row_ref), (phase_in, phase), (probe_in, probe),
             (right_in, right), (measured_in, measured)]
        )
    ]
    obj_loads = [
        pltpu.make_async_copy(obj_in.at[:, layer], obj.at[:, layer], obj_sem.at[layer])
        for layer in range(layers)
    ]
    loads[0].start()
    for copy in obj_loads + loads[1:]:
        copy.start()

    loads[0].wait()
    starts = [prior * count, tile * count + half, tile * count, prior * count + half]
    for slot, start in enumerate(starts):
        for q in range(half):
            place[slot, q] = one_hot((window, columns), 1, col_ref[start + q])

    def cut(layer, pick, target):
        for c in range(2):
            target[c] = lax.dot_general(
                obj[c, layer], pick, (((1,), (1,)), ((), ())), preferred_element_type=F32
            ).astype(BF16)

    def low_copy(layer, q, c):
        return remote(
            cut_low.at[layer, q, c], both.at[side * layers + layer, q, c, 1],
            low_send.at[layer, q, c], part_recv.at[side * layers + layer, q, c],
            tile=prior, slab=2 * group,
        )

    def high_copy(layer, q, c):
        return remote(
            cut_high.at[layer, q, c], both.at[side * layers + layer, q, c, 0],
            high_send.at[layer, q, c], part_recv.at[side * layers + layer, q, c],
            tile=after, slab=2 * group + 1,
        )

    def give_copy(layer, q, c):
        return remote(
            cut_give.at[layer, q, c], both.at[side * layers + layer, q, c, 1 - side],
            give_send.at[layer, q, c], give_recv.at[layer, q, c], slab=partner,
        )

    def seen_copy(q):
        return remote(
            measured.at[half + q], seen.at[q], seen_send.at[q], seen_recv.at[q], tile=after
        )

    for layer in range(layers):
        obj_loads[layer].wait()
        for q in range(half):
            cut(layer, place[0, q], cut_low.at[layer, q])
            cut(layer, place[1, q], cut_high.at[layer, q])
    pl.semaphore_wait(barrier, len(greeted))
    for layer in range(layers):
        for q, c in pieces:
            low_copy(layer, q, c).start()
            high_copy(layer, q, c).start()
    for layer in range(layers):
        for q in range(half):
            cut(layer, place[3 - side, q], cut_give.at[layer, q])
        for q, c in pieces:
            give_copy(layer, q, c).start()
    for layer in range(layers):
        for q, c in pieces:
            both[side * layers + layer, q, c, side] = lax.dot_general(
                obj[c, layer], place[2 + side, q], (((1,), (1,)), ((), ())),
                preferred_element_type=F32,
            ).astype(BF16)

    for copy in loads[1:]:
        copy.wait()
    my_rows = [row_ref[base * count + side * half + q] for q in range(half)]
    prop[0] = jnp.cos(phase[...])
    prop[1] = jnp.sin(phase[...])

    def cross_copy(step, at, c):
        block = patches.at[first_own + at, c]
        return remote(
            block, block, cross_send.at[step - 1, at, c], cross_recv.at[step - 1, at, c],
            slab=lax.rem(group + step, groups) * 2 + side,
        )

    def cross_arrival(step, j, at, c):
        block = patches.at[j, c]
        return remote(
            block, block, cross_send.at[step - 1, at, c], cross_recv.at[step - 1, at, c],
            slab=lax.rem(group + step, groups) * 2 + side,
        )

    def take_rows(at, c):
        owner, layer = at // layers, lax.rem(at, layers)
        for q in range(half):
            remote(
                cut_low.at[0, q, c], both.at[at, q, c, 1 - side],
                low_send.at[0, q, c], part_recv.at[at, q, c], slab=partner,
            ).wait_recv()

        @pl.when(owner != side)
        def _():
            for q in range(half):
                remote(
                    cut_give.at[0, q, c], both.at[at, q, c, side],
                    give_send.at[0, q, c], give_recv.at[layer, q, c], slab=partner,
                ).wait_recv()

        for q in range(half):
            pick = one_hot((window, 2 * window), 1, my_rows[q])
            rows = both[at, q, c].reshape(2 * window, window)
            patches[first_own + at, c, q] = jnp.dot(
                pick, rows, preferred_element_type=F32
            ).astype(BF16)
        for step in range(1, groups):
            cross_copy(step, at, c).start()

    @pl.when(group > 0)
    def _():
        for layer in range(layers):
            for c in range(2):
                for owner in range(2):
                    take_rows(owner * layers + layer, c)

    def arrive(j):
        of_group, at = j // owned, lax.rem(j, owned)
        step = lax.rem(group - of_group + groups, groups)

        @pl.when(of_group != group)
        def _():
            for c in range(2):
                cross_arrival(step, j, at, c).wait_recv()

    run = functools.partial(transform, right=right, window=window)
    for q in range(half):
        for c in range(2):
            psi[0, q, c] = probe[c].astype(F32)

    def patch(j):
        return [(patches[j, 0, q].astype(F32), patches[j, 1, q].astype(F32)) for q in range(half)]

    def pair(ref, q):
        return ref[q, 0], ref[q, 1]

    def waves(j):
        return [(psi[j, q, 0], psi[j, q, 1]) for q in range(half)]

    def forward(j, carried):
        @pl.when((group == 0) & (j < layers))
        def _():
            for c in range(2):
                take_rows(j, c)
                take_rows(j + layers, c)

        @pl.when((side == 1) & (j == layers))
        def _():
            for q in range(half):
                seen_copy(q).start()

        arrive(j)
        chi = [times(a, b) for a, b in zip(waves(j), patch(j))]
        moved = run(chi)
        pace = (prop[0], prop[1])
        back = run([conj(times(pace, f)) for f in moved])
        for q in range(half):
            psi[j + 1, q, 0] = back[q][0]
            psi[j + 1, q, 1] = -back[q][1]
        return carried

    lax.fori_loop(0, last, forward, 0)

    @pl.when(side == 0)
    def _():
        for q in range(half):
            seen[q] = measured[q]

    @pl.when(side == 1)
    def _():
        for q in range(half):
            seen_copy(q).wait_recv()

    arrive(last)
    chi = [times(a, b) for a, b in zip(waves(last), patch(last))]
    far = run(chi)
    shaped = []
    for q, (re, im) in enumerate(far):
        misfit = re * re + im * im - seen[q]
        shaped.append((misfit * re, -(misfit * im)))
    grad = [conj(f) for f in run(shaped)]
    for q in range(half):
        work[q, 0], work[q, 1] = grad[q]

    def near_copy(at, q):
        return remote(
            stage.at[at, q, side], landed.at[lax.rem(at, layers), 2 + side, q],
            near_send.at[lax.rem(at, layers), q], near_recv.at[lax.rem(at, layers), q], slab=partner,
        )

    def far_copy(at, q):
        return remote(
            stage.at[at, q, 1 - side], landed.at[lax.rem(at, layers), side, q],
            far_send.at[at, q], far_recv.at[side, lax.rem(at, layers), q],
            tile=beyond, slab=2 * group + at // layers,
        )

    def own_term(j):
        @pl.when(j < first_own + owned)
        def _():
            at = j - first_own
            for q in range(half):
                term = jnp.concatenate(
                    conj_times((psi[j, q, 0], psi[j, q, 1]), pair(work, q)), axis=1
                )
                pick = one_hot((2 * window, window), 0, my_rows[q])
                placed = jnp.dot(
                    pick, term.astype(BF16), preferred_element_type=F32
                ).astype(BF16)
                for part in range(2):
                    rows = placed[part * window : (part + 1) * window]
                    stage[at, q, part, 0], stage[at, q, part, 1] = halves(rows, window)
                far_copy(at, q).start()

            @pl.when(at // layers != side)
            def _():
                for q in range(half):
                    near_copy(at, q).start()

    def backward(i, carried):
        j = last - i
        own_term(j)
        grads = [pair(work, q) for q in range(half)]
        inner = [conj_times(a, b) for a, b in zip(patch(j), grads)]
        moved = run(inner)
        pace = (prop[0], prop[1])
        back = run([conj(conj_times(pace, f)) for f in moved])
        for q in range(half):
            work[q, 0] = back[q][0]
            work[q, 1] = -back[q][1]
        return carried

    lax.fori_loop(0, last - first_own, backward, 0)
    own_term(first_own)

    def far_arrival(layer, of_side, q):
        return remote(
            stage.at[0, q, 0], landed.at[layer, of_side, q],
            far_send.at[0, q], far_recv.at[of_side, layer, q], slab=partner,
        )

    def near_arrival(layer, q):
        return remote(
            stage.at[0, q, 0], landed.at[layer, 3 - side, q],
            near_send.at[layer, q], near_recv.at[layer, q], slab=partner,
        )

    def out_copy(c, layer):
        return pltpu.make_async_copy(total.at[c, layer], out.at[c, layer], out_sem.at[c, layer])

    all_place = place[...].reshape(4 * half * window, columns)
    for layer in reversed(range(layers)):
        for q in range(half):
            landed[layer, 2 + side, q] = stage[side * layers + layer, q, side]
            near_arrival(layer, q).wait_recv()
            for of_side in range(2):
                far_arrival(layer, of_side, q).wait_recv()
        for c in range(2):
            blocks = [landed[layer, slot, q, c] for slot in range(4) for q in range(half)]
            total[c, layer] = jnp.dot(
                jnp.concatenate(blocks, axis=1), all_place, preferred_element_type=F32
            ).astype(total.dtype)
            out_copy(c, layer).start()

    @pl.when(side == 1)
    def _():
        for q in range(half):
            seen_copy(q).wait_send()

    for layer in range(layers):
        for q, c in pieces:
            low_copy(layer, q, c).wait_send()
            high_copy(layer, q, c).wait_send()
            give_copy(layer, q, c).wait_send()
        for q in range(half):
            near_copy((1 - side) * layers + layer, q).wait_send()
    for at in range(owned):
        for q in range(half):
            far_copy(at, q).wait_send()
        for c in range(2):
            for step in range(1, groups):
                cross_copy(step, at, c).wait_send()
    for layer in range(layers):
        for c in range(2):
            out_copy(c, layer).wait()


def body(object_field, probe_wave, prop_phase, intensity, patch_rows, patch_cols):
    window = probe_wave.shape[1]
    layers, columns = object_field.shape[1], object_field.shape[3]
    half = intensity.shape[0] // 2
    tiles, sections = lax.axis_size("tile"), lax.axis_size("slab")
    slices = sections * layers
    groups = sections // 2
    owned = 2 * layers
    right = fourier_parts(window)
    block = (window, window)
    dma = pltpu.SemaphoreType.DMA
    return pl.pallas_call(
        functools.partial(kernel, tiles, sections),
        out_shape=jax.ShapeDtypeStruct(object_field.shape, BF16),
        in_specs=[pl.BlockSpec(memory_space=pl.ANY)] * 7,
        out_specs=pl.BlockSpec(memory_space=pl.ANY),
        scratch_shapes=[
            pltpu.SMEM(patch_rows.shape, jnp.int32),
            pltpu.SMEM(patch_cols.shape, jnp.int32),
            pltpu.VMEM(object_field.shape, BF16),
            pltpu.VMEM(probe_wave.shape, BF16),
            pltpu.VMEM(prop_phase.shape, F32),
            pltpu.VMEM(intensity.shape, F32),
            pltpu.VMEM((4, half, window, columns), BF16),
            pltpu.VMEM((layers, half, 2) + block, BF16),
            pltpu.VMEM((layers, half, 2) + block, BF16),
            pltpu.VMEM((layers, half, 2) + block, BF16),
            pltpu.VMEM((owned, half, 2, 2) + block, BF16),
            pltpu.VMEM((slices, 2, half) + block, BF16),
            pltpu.VMEM((slices, half, 2) + block, F32),
            pltpu.VMEM((half, 2) + block, F32),
            pltpu.VMEM((2,) + block, F32),
            pltpu.VMEM((half,) + block, F32),
            pltpu.VMEM((owned, half, 2, 2) + block, BF16),
            pltpu.VMEM((layers, 4, half, 2) + block, BF16),
            pltpu.VMEM(right.shape, BF16),
            pltpu.VMEM(object_field.shape, BF16),
            dma((6,)),
            dma((layers,)),
            dma((2, layers)),
            dma((layers, half, 2)),
            dma((layers, half, 2)),
            dma((layers, half, 2)),
            dma((owned, half, 2)),
            dma((layers, half, 2)),
            dma((groups - 1, owned, 2)),
            dma((groups - 1, owned, 2)),
            dma((half,)),
            dma((half,)),
            dma((layers, half)),
            dma((layers, half)),
            dma((owned, half)),
            dma((2, layers, half)),
        ],
        compiler_params=pltpu.CompilerParams(
            collective_id=0, has_side_effects=True, vmem_limit_bytes=60 * 1024 * 1024
        ),
    )(
        patch_rows, patch_cols, object_field, probe_wave, prop_phase, intensity,
        jnp.asarray(right),
    )


def solution(mesh):
    return jax.shard_map(
        body,
        mesh=mesh,
        in_specs=(P(None, "slab", "tile", None), P(), P(), P("tile", None, None), P(), P()),
        out_specs=P(None, "slab", "tile", None),
        check_vma=False,
    )
```
